128 devices in a mesh: pair: 32 (over z, y, x_lo), chol: 4 (over x_hi, core).
Axes of the slice: x: 4 (x_hi: 2, x_lo: 2; x = x_hi * 2 + x_lo), y: 4, z: 4, core: 2. Of those that a mesh axis runs over, the one named last changes fastest.
Arguments:
- left_vectors: bfloat16 [8, 160, 800], P(None, 'pair'), may hold values from -6 to 6
- chol_factors: bfloat16 [160, 800, 2560], P('pair', None, 'chol'), may hold values from -0.046875 to 0.046875
- eps_occ: float32 [160], P('pair'), may hold values from -1.5 to -0.3
- eps_vir: float32 [800], replicated, may hold values from 0.2 to 3
Outputs:
- left_sigma: float32 [8, 160, 800], P(None, 'pair')
The draws below stay inside these ranges and needn't reach their ends.
All inputs are finite; a program needn't handle non-finite values.
Results may differ from the reference program's by a relative error of at most 0.0016.
Values may be sent and summed in bfloat16 or wider, within the bound.
No kernel may reach another device: no remote copies, remote signals or barrier semaphores. Data moves between devices by JAX's collectives and lax.ppermute only.
A program may use at most 64 MiB of HBM per device.

```python
import jax
import jax.numpy as jnp
from jax import lax

OCC = 160
VIR = 800
NAUX = 2560
ROOTS = 8


def steps_of(rng, shape, cuts, smallest, largest):
    loudness = 1.0
    for axis_at, blocks in cuts:
        steps = jax.random.uniform(jax.random.fold_in(jax.random.fold_in(rng, 6), axis_at), (blocks,), jnp.float32, smallest / len(cuts), largest / len(cuts))
        loudness = loudness * jnp.repeat(jnp.exp(steps), shape[axis_at] // blocks).reshape((-1,) + (1,) * (len(shape) - 1 - axis_at))
    return loudness


def centred(key, dims, width, limit, shards=(), kind=jnp.bfloat16):
    factor_of = steps_of(key, dims, shards, -0.22, 0.18) if shards else 1.0
    entries = jax.random.normal(key, dims, jnp.float32) * width * factor_of
    return jnp.minimum(jnp.maximum(entries, -limit), limit).astype(kind)


def setup_inputs(seed: int = 0) -> dict:
    keys = jax.random.split(jax.random.key(seed), 5)
    return {
        "left_vectors": centred(keys[0], (ROOTS, OCC, VIR), 1.0, 6.0, ((1, 32),)),
        "chol_factors": centred(keys[1], (OCC, VIR, NAUX), ((OCC * VIR * NAUX) ** -0.25), 0.046875, ((0, 32), (2, 4))),
        "eps_occ": jnp.clip(-1.5 + 1.2 * jax.random.uniform(keys[2], (OCC,), jnp.float32) ** steps_of(keys[2], (OCC,), ((0, 32),), -0.2, 0.2), -1.5, -0.3),
        "eps_vir": jnp.clip(jax.random.uniform(keys[3], (VIR,), jnp.float32, 0.2, 3.0), 0.2, 3.0),
    }


def reference(left_vectors, chol_factors, eps_occ, eps_vir):
    occ_count, vir_count, aux_count = chol_factors.shape
    root_count = left_vectors.shape[0]
    flat_pairs = chol_factors.reshape(occ_count * vir_count, aux_count)
    coul_vec = jnp.dot(left_vectors.reshape(root_count, occ_count * vir_count), flat_pairs, preferred_element_type=jnp.float32).astype(jnp.bfloat16)
    coulomb = jnp.dot(flat_pairs, coul_vec.T, preferred_element_type=jnp.float32).T.reshape(root_count, occ_count, vir_count)

    def per_root(left_one):
        def one_slab(occ_slab):
            return jnp.dot(left_one, occ_slab, preferred_element_type=jnp.float32).astype(jnp.bfloat16)
        z_inter = lax.map(one_slab, chol_factors)

        def add_slab(total, pieces):
            z_column, factor_slab = pieces
            return total + jnp.dot(z_column, factor_slab.T, preferred_element_type=jnp.float32), None

        start = jnp.zeros((occ_count, vir_count), jnp.float32)
        total, unused = lax.scan(add_slab, start, (jnp.swapaxes(z_inter, 0, 1), chol_factors))
        return total

    exchange_term = lax.map(per_root, left_vectors)
    diagonal_part = (eps_vir[None, None, :] - eps_occ[None, :, None]) * left_vectors.astype(jnp.float32)
    return diagonal_part + 2.0 * coulomb - exchange_term
```

```python
import jax
import jax.numpy as jnp
from jax import lax
from jax.sharding import PartitionSpec as P

CORE_SWAP = [(0, 1), (1, 0), (2, 3), (3, 2)]
FAR_SWAP = [(0, 2), (2, 0), (1, 3), (3, 1)]


def exchange(blocks):
    return lax.all_to_all(blocks, "pair", split_axis=0, concat_axis=0, tiled=True)


def body(left_vectors, chol_factors, eps_occ, eps_vir):
    roots, occ_local, vir = left_vectors.shape
    aux_local = chol_factors.shape[2]
    ranks = lax.axis_size("pair")
    aux_own = aux_local // ranks
    occ = occ_local * ranks
    half = roots // 2
    core = lax.rem(lax.axis_index("chol"), 2)

    by_aux = chol_factors.reshape(occ_local * vir, aux_local).T
    by_aux = exchange(by_aux.reshape(ranks, aux_own, occ_local * vir))
    factors = by_aux.reshape(ranks, aux_own, occ_local, vir)

    own_half = lax.dynamic_slice_in_dim(left_vectors, core * half, half, 0)
    mine = exchange(jnp.broadcast_to(own_half[None], (ranks, half, occ_local, vir)))
    other = lax.ppermute(mine, "chol", CORE_SWAP)
    lefts = jnp.where(
        core == 0,
        jnp.concatenate([mine, other], axis=1),
        jnp.concatenate([other, mine], axis=1),
    )

    coul_part = jnp.einsum(
        "ria,iap->rp", left_vectors, chol_factors, preferred_element_type=jnp.float32
    )
    coul_part = exchange(coul_part.reshape(roots, ranks, aux_own).transpose(1, 0, 2))
    coul_own = jnp.sum(coul_part, axis=0).astype(jnp.bfloat16)
    coul_vec = exchange(jnp.broadcast_to(coul_own[None], (ranks, roots, aux_own)))
    coul_vec = coul_vec.transpose(1, 0, 2).reshape(roots, aux_local)
    coulomb = jnp.einsum("iap,rp->ria", chol_factors, coul_vec, preferred_element_type=jnp.float32)

    z_inter = jnp.einsum(
        "dpib,erjb->rdipej", factors, lefts, preferred_element_type=jnp.float32
    ).astype(jnp.bfloat16)
    partial_all = jnp.einsum(
        "rdipej,epja->dria", z_inter, factors, preferred_element_type=jnp.float32
    )

    keep = lax.dynamic_slice_in_dim(partial_all, core * half, half, 1)
    give = lax.dynamic_slice_in_dim(partial_all, (1 - core) * half, half, 1)
    keep = keep + lax.ppermute(give, "chol", CORE_SWAP)
    pieces = exchange(keep.astype(jnp.bfloat16))
    exch = jnp.sum(pieces.astype(jnp.float32), axis=0)

    coul_keep = lax.dynamic_slice_in_dim(coulomb, core * half, half, 0)
    coul_give = lax.dynamic_slice_in_dim(coulomb, (1 - core) * half, half, 0)
    coul_keep = coul_keep + lax.ppermute(coul_give, "chol", CORE_SWAP)
    part = 2.0 * coul_keep - exch
    part = part + lax.ppermute(part, "chol", FAR_SWAP)
    rest = lax.ppermute(part, "chol", CORE_SWAP)
    summed = jnp.where(
        core == 0,
        jnp.concatenate([part, rest], axis=0),
        jnp.concatenate([rest, part], axis=0),
    )
    diagonal_part = (eps_vir[None, None, :] - eps_occ[None, :, None]) * left_vectors.astype(
        jnp.float32
    )
    return diagonal_part + summed


def solution(mesh):
    placed = (P(None, "pair", None), P("pair", None, "chol"), P("pair"), P())
    return jax.shard_map(
        body, mesh=mesh, in_specs=placed, out_specs=P(None, "pair", None), check_vma=False
    )
```

```python
import functools

import jax
import jax.numpy as jnp
from jax import lax
from jax.experimental import pallas as pl
from jax.experimental.pallas import tpu as pltpu
from jax.sharding import PartitionSpec as P

CORE_SWAP = [(0, 1), (1, 0), (2, 3), (3, 2)]
FAR_SWAP = [(0, 2), (2, 0), (1, 3), (3, 1)]
LANES = 128
FIRST = 12
CHUNK = 1024
VMEM = pl.BlockSpec(memory_space=pltpu.VMEM)
HIGH = 48 * 1024 * 1024
NT = (((1,), (1,)), ((), ()))


def exchange(blocks):
    return lax.all_to_all(blocks, "pair", split_axis=0, concat_axis=0, tiled=True)


def up(value, unit):
    return pl.cdiv(value, unit) * unit


def iota(shape, axis):
    return lax.broadcasted_iota(jnp.int32, shape, axis)


def one_hot(flag):
    return jnp.where(flag, 1.0, 0.0).astype(jnp.bfloat16)


def dot(a, b):
    return jnp.dot(a, b, preferred_element_type=jnp.float32)


def pack_kernel(dims, factors_ref, left_ref, first_ref, second_ref, sums):
    ranks, share, rows, roots = dims
    half = roots // 2
    rest = share - FIRST
    pitch = FIRST + half
    cut = ranks * FIRST
    aux = ranks * share
    k = pl.program_id(0)
    last = pl.cdiv(rows, CHUNK) - 1

    row, col = iota((ranks * pitch, cut), 0), iota((ranks * pitch, cut), 1)
    pick = one_hot((row % pitch < FIRST) & (col == row // pitch * FIRST + row % pitch))
    row, col = iota((ranks * pitch, roots), 0), iota((ranks * pitch, roots), 1)
    lay = one_hot(row % pitch == FIRST + col)
    keep = one_hot(iota((aux - cut, aux - cut), 0) == iota((aux - cut, aux - cut), 1))

    def some(size):
        block = factors_ref[:size, :]
        left = left_ref[:, :size]
        moved = lax.dot_general(pick, block[:, :cut], NT, preferred_element_type=jnp.float32)
        first_ref[:, :size] = (moved + dot(lay, left)).astype(jnp.bfloat16)
        moved = lax.dot_general(keep, block[:, cut:], NT, preferred_element_type=jnp.float32)
        second_ref[:, :size] = moved.astype(jnp.bfloat16)
        return dot(left, block)

    @pl.when(k == 0)
    def _():
        sums[...] = some(CHUNK)

    @pl.when((k > 0) & (k < last))
    def _():
        sums[...] += some(CHUNK)

    @pl.when(k == last)
    def _():
        size = rows - last * CHUNK
        left_over = sums[...] + some(size)
        row, col = iota((ranks * pitch, roots), 0), iota((ranks * pitch, roots), 1)
        lay_root = one_hot(row % pitch == col)
        row, col = iota((ranks * pitch, aux), 0), iota((ranks * pitch, aux), 1)
        owner = jnp.where(col < cut, col // FIRST, (col - cut) // rest)
        mine = owner == row // pitch
        spare = CHUNK - size
        row, col = iota((aux, spare), 0), iota((aux, spare), 1)
        slot = jnp.where(row < cut, row % FIRST, FIRST + (row - cut) % rest)
        extra = jnp.zeros((ranks * pitch, spare), jnp.float32)
        for t in range(3):
            term = left_over.astype(jnp.bfloat16)
            left_over = left_over - term.astype(jnp.float32)
            spread = jnp.where(mine, dot(lay_root, term), 0.0).astype(jnp.bfloat16)
            extra = extra + dot(spread, one_hot(col == t * share + slot))
        first_ref[:, size:] = extra.astype(jnp.bfloat16)
        second_ref[:, size:] = jnp.zeros((ranks * rest, spare), jnp.bfloat16)


def pack(factors, lefts, dims):
    ranks, share, rows, roots = dims
    pitch = FIRST + roots // 2
    rest = share - FIRST
    steps = pl.cdiv(rows, CHUNK)
    return pl.pallas_call(
        functools.partial(pack_kernel, dims),
        grid=(steps,),
        in_specs=[
            pl.BlockSpec((CHUNK, ranks * share), lambda k: (k, 0)),
            pl.BlockSpec((roots, CHUNK), lambda k: (0, k)),
        ],
        out_specs=[
            pl.BlockSpec((ranks * pitch, CHUNK), lambda k: (0, k)),
            pl.BlockSpec((ranks * rest, CHUNK), lambda k: (0, k)),
        ],
        out_shape=[
            jax.ShapeDtypeStruct((ranks * pitch, steps * CHUNK), jnp.bfloat16),
            jax.ShapeDtypeStruct((ranks * rest, steps * CHUNK), jnp.bfloat16),
        ],
        scratch_shapes=[pltpu.VMEM((roots, ranks * share), jnp.float32)],
        compiler_params=pltpu.CompilerParams(vmem_limit_bytes=HIGH),
    )(factors, lefts)


def coul_kernel(dims, got_ref, send_ref, out_ref):
    ranks, share, rows, roots = dims
    pitch = FIRST + roots // 2
    rest = share - FIRST
    start = rows % LANES
    row, col = iota((roots, ranks * pitch), 0), iota((roots, ranks * pitch), 1)
    sums = dot(one_hot(col % pitch == row), got_ref[...])
    turn = LANES - share
    once = pltpu.roll(sums, turn, 1)
    sums = sums + once + pltpu.roll(once, turn, 1)
    row, col = iota((ranks * rest, roots), 0), iota((ranks * rest, roots), 1)
    laid = dot(one_hot(row % rest == col), sums.astype(jnp.bfloat16)).astype(jnp.bfloat16)
    lane = iota((ranks * rest, LANES), 1)
    out_ref[...] = jnp.where(lane < start, send_ref[...], laid)


def coul_round(got, send, dims):
    ranks, share, rows, roots = dims
    at = rows // LANES
    return pl.pallas_call(
        functools.partial(coul_kernel, dims),
        grid=(1,),
        in_specs=[
            pl.BlockSpec((got.shape[0], LANES), lambda k: (0, at)),
            pl.BlockSpec((send.shape[0], LANES), lambda k: (0, at)),
        ],
        out_specs=pl.BlockSpec((send.shape[0], LANES), lambda k: (0, at)),
        out_shape=jax.ShapeDtypeStruct(send.shape, send.dtype),
        input_output_aliases={1: 0},
    )(got, send)


def left_kernel(dims, got_ref, out_ref):
    ranks, occ_local, vir, half = dims
    pitch = FIRST + half
    main = ranks * (occ_local - 1)
    for r in range(half):
        row, col = iota((ranks, ranks * pitch), 0), iota((ranks, ranks * pitch), 1)
        turn = one_hot(col == row * pitch + FIRST + r)
        for i in range(occ_local):
            part = dot(turn, got_ref[:, i * vir : (i + 1) * vir]).T.astype(jnp.bfloat16)
            to = r * main + i * ranks if i < occ_local - 1 else half * main + r * ranks
            out_ref[:, to : to + ranks] = part


def left_half(got, dims):
    ranks, occ_local, vir, half = dims
    return pl.pallas_call(
        functools.partial(left_kernel, dims),
        in_specs=[VMEM],
        out_specs=VMEM,
        out_shape=jax.ShapeDtypeStruct((vir, half * ranks * occ_local), jnp.bfloat16),
        compiler_params=pltpu.CompilerParams(vmem_limit_bytes=24 * 1024 * 1024),
    )(got)


def slab_kernel(dims, final, recv_ref, mine_ref, other_ref, *refs):
    ranks, share, pitch, occ_local, vir, roots = dims
    if final:
        total_ref, keep_ref, give_ref, left, rows_z, rows_e, zed = refs
    else:
        out_ref, left, rows_z, rows_e, zed = refs
    occ = ranks * occ_local
    main = occ - ranks
    packed = main // ranks
    half = roots // 2

    @pl.when(pl.program_id(0) == 0)
    def _():
        for h, ref in enumerate((mine_ref, other_ref)):
            left[:, h * half * main : (h + 1) * half * main] = ref[:, : half * main]
            to = roots * main + h * half * ranks
            left[:, to : to + half * ranks] = ref[:, half * main :]

        group = min(ranks, 256 // pitch)
        row, col = iota((group * share, group * pitch), 0), iota((group * share, group * pitch), 1)
        turn = one_hot(col == (row % group) * pitch + row // group)
        for at in range(ranks // group):
            for i in range(occ_local):
                part = recv_ref[
                    at * group * pitch : (at + 1) * group * pitch, i * vir : (i + 1) * vir
                ]
                part = dot(turn, part).astype(jnp.bfloat16)
                for s in range(share):
                    rows = part[s * group : (s + 1) * group]
                    to = s * occ + i * ranks + at * group
                    rows_z[to : to + group, :] = rows
                    if i < occ_local - 1:
                        to = s * main + i * ranks + at * group
                    else:
                        to = share * main + s * ranks + at * group
                    rows_e[to : to + group, :] = rows

        place = iota((occ, main), 1) // ranks

        def some_vectors(k, carry):
            at = pl.multiple_of(k * packed * occ, packed * occ)
            z = dot(rows_z[pl.ds(at, packed * occ), :], left[...]).astype(jnp.bfloat16)
            for r in range(roots):
                low = roots * main + (r // packed) * main
                rest = jnp.zeros((occ, main), jnp.bfloat16)
                for s in range(packed):
                    zs = z[s * occ : (s + 1) * occ]
                    to = pl.multiple_of(k * packed * main, packed * main) + s * main
                    zed[r * occ : (r + 1) * occ, pl.ds(to, main)] = zs[:, r * main : (r + 1) * main]
                    turned = zs[:, low : low + main]
                    shift = (s - r % packed) % packed * ranks
                    if shift:
                        turned = pltpu.roll(turned, shift, 1)
                    rest = jnp.where(place == s, turned, rest)
                to = pl.multiple_of(share * main + k * main, main)
                zed[r * occ : (r + 1) * occ, pl.ds(to, main)] = rest
            return carry

        lax.fori_loop(0, share // packed, some_vectors, 0)

    if not final:
        step = out_ref.shape[0]
        at = pl.multiple_of(pl.program_id(0) * step, step)
        out_ref[:, :vir] = dot(zed[pl.ds(at, step), :], rows_e[...])
        return
    step = half * occ

    @pl.when(pl.program_id(0) == 0)
    def _():
        keep_ref[:, :vir] = total_ref[:, :vir] + dot(zed[:step, :], rows_e[...])

    @pl.when(pl.program_id(0) == 1)
    def _():
        give_ref[:, :vir] = total_ref[:, :vir] + dot(zed[step:, :], rows_e[...])


def slab_product(recv, mine, other, total, dims):
    ranks, share, pitch, occ_local, vir, roots = dims
    occ = ranks * occ_local
    width = up(vir, LANES)
    final = total is not None
    steps = 2 if final else 4
    rows = roots * occ // steps
    args = [recv, mine, other] + ([total] if final else [])
    block = pl.BlockSpec((rows, width), lambda k: (k, 0))
    fixed = pl.BlockSpec((rows, width), lambda k: (0, 0))
    shape = jax.ShapeDtypeStruct((rows if final else roots * occ, width), jnp.float32)
    return pl.pallas_call(
        functools.partial(slab_kernel, dims, final),
        grid=(steps,),
        in_specs=[VMEM, VMEM, VMEM] + ([block] if final else []),
        out_specs=[fixed, fixed] if final else block,
        out_shape=[shape, shape] if final else shape,
        scratch_shapes=[
            pltpu.VMEM((vir, roots * occ), jnp.bfloat16),
            pltpu.VMEM((share * occ, vir), jnp.bfloat16),
            pltpu.VMEM((share * occ, vir), jnp.bfloat16),
            pltpu.VMEM((roots * occ, share * occ), jnp.bfloat16),
        ],
        compiler_params=pltpu.CompilerParams(vmem_limit_bytes=HIGH),
        cost_estimate=pl.CostEstimate(
            flops=4 * share * occ * roots * occ * vir,
            transcendentals=0,
            bytes_accessed=2 * share * occ * vir + 8 * roots * occ * vir,
        ),
    )(*args)


def merge_kernel(keep_ref, other_ref, out_ref, tiles):
    ranks, occ_local, half, vir = out_ref.shape
    occ = ranks * occ_local
    for t in range(tiles.shape[0]):
        at = slice(t * LANES, (t + 1) * LANES)
        tiles[t] = keep_ref[:, at] + other_ref[:, at]
    for d in range(ranks):
        for i in range(occ_local):
            for t in range(tiles.shape[0]):
                at = t * LANES
                size = min(LANES, vir - at)
                rows = tiles[t, pl.ds(i * ranks + d, half, stride=occ), :]
                out_ref[d, i, :, at : at + size] = rows[:, :size].astype(jnp.bfloat16)


def merge(keep, other, shape):
    rows, width = keep.shape
    return pl.pallas_call(
        merge_kernel,
        in_specs=[VMEM, VMEM],
        out_specs=VMEM,
        out_shape=jax.ShapeDtypeStruct(shape, jnp.bfloat16),
        scratch_shapes=[pltpu.VMEM((width // LANES, rows, LANES), jnp.float32)],
        compiler_params=pltpu.CompilerParams(vmem_limit_bytes=24 * 1024 * 1024),
    )(keep, other)


def body(left_vectors, chol_factors, eps_occ, eps_vir):
    roots, occ_local, vir = left_vectors.shape
    aux_local = chol_factors.shape[2]
    ranks = lax.axis_size("pair")
    share = aux_local // ranks
    rest = share - FIRST
    rows = occ_local * vir
    occ = occ_local * ranks
    half = roots // 2
    core = lax.rem(lax.axis_index("chol"), 2)
    dims = (ranks, share, rows, roots)

    turned = jnp.where(
        core == 0, left_vectors, jnp.concatenate([left_vectors[half:], left_vectors[:half]], axis=0)
    )
    flat = turned.reshape(roots, rows)
    first_send, second_send = pack(
        chol_factors.reshape(rows, aux_local),
        jnp.pad(flat, ((0, 0), (0, up(rows, CHUNK) - rows))),
        dims,
    )

    pitch = FIRST + half
    first = exchange(first_send.reshape(ranks, pitch, -1)).reshape(ranks * pitch, -1)
    second_send = coul_round(first, second_send, dims)
    second = exchange(second_send.reshape(ranks, rest, -1)).reshape(ranks * rest, -1)
    mine = left_half(first, (ranks, occ_local, vir, half))
    other = lax.ppermute(mine, "chol", CORE_SWAP)

    total = slab_product(first, mine, other, None, (ranks, FIRST, pitch, occ_local, vir, roots))
    keep, give = slab_product(
        second, mine, other, total, (ranks, rest, rest, occ_local, vir, roots)
    )

    merged = merge(keep, lax.ppermute(give, "chol", CORE_SWAP), (ranks, occ_local, half, vir))
    merged, second = lax.optimization_barrier((merged, second))
    pieces = exchange(merged)
    exch = jnp.sum(pieces.astype(jnp.float32), axis=0).transpose(1, 0, 2)

    coul_vec = second[:, rows : rows + share].reshape(ranks, roots, share).transpose(1, 0, 2)
    coul_vec = jnp.concatenate(
        [
            coul_vec[:, :, :FIRST].reshape(roots, ranks * FIRST),
            coul_vec[:, :, FIRST:].reshape(roots, ranks * rest),
        ],
        axis=1,
    )
    coulomb = jnp.einsum("iap,rp->ria", chol_factors, coul_vec, preferred_element_type=jnp.float32)
    coul_keep = coulomb[:half] + lax.ppermute(coulomb[half:], "chol", CORE_SWAP)

    part = 2.0 * coul_keep - exch
    part = part + lax.ppermute(part, "chol", FAR_SWAP)
    rest_part = lax.ppermute(part, "chol", CORE_SWAP)
    summed = jnp.where(
        core == 0,
        jnp.concatenate([part, rest_part], axis=0),
        jnp.concatenate([rest_part, part], axis=0),
    )
    diagonal_part = (eps_vir[None, None, :] - eps_occ[None, :, None]) * left_vectors.astype(
        jnp.float32
    )
    return diagonal_part + summed


def solution(mesh):
    placed = (P(None, "pair", None), P("pair", None, "chol"), P("pair"), P())
    return jax.shard_map(
        body, mesh=mesh, in_specs=placed, out_specs=P(None, "pair", None), check_vma=False
    )
```

```python
import functools

import jax
import jax.numpy as jnp
from jax import lax
from jax.experimental import pallas as pl
from jax.experimental.pallas import tpu as pltpu
from jax.sharding import PartitionSpec as P


CORE_SWAP = [(0, 1), (1, 0), (2, 3), (3, 2)]
FAR_SWAP = [(0, 2), (2, 0), (1, 3), (3, 1)]
LANES = 128
FIRST = 12
CHUNK = 1024
VMEM = pl.BlockSpec(memory_space=pltpu.VMEM)
HBM = pl.BlockSpec(memory_space=pl.ANY)
MIB = 1024 * 1024
HIGH = 48 * MIB
VLIM1 = 60 * MIB
VLIM2 = 40 * MIB
VLIM3 = 16 * MIB
NT = (((1,), (1,)), ((), ()))


def exchange(blocks):
    return lax.all_to_all(blocks, "pair", split_axis=0, concat_axis=0, tiled=True)


def up(value, unit):
    return pl.cdiv(value, unit) * unit


def iota(shape, axis):
    return lax.broadcasted_iota(jnp.int32, shape, axis)


def one_hot(flag):
    return jnp.where(flag, 1.0, 0.0).astype(jnp.bfloat16)


def dot(a, b):
    return jnp.dot(a, b, preferred_element_type=jnp.float32)


def pack_kernel(
    dims, core_ref, factors_ref, left_ref, first_ref, second_ref, sums, pick, lay, keep
):
    ranks, share, rows, roots = dims
    half = roots // 2
    rest = share - FIRST
    pitch = FIRST + half
    cut = ranks * FIRST
    aux = ranks * share
    k = pl.program_id(0)
    last = pl.cdiv(rows, CHUNK) - 1

    def some(size):
        block = factors_ref[:size, :]
        left = left_ref[:, :size]
        moved = lax.dot_general(pick[...], block[:, :cut], NT, preferred_element_type=jnp.float32)
        first_ref[:, :size] = (moved + dot(lay[...], left)).astype(jnp.bfloat16)
        moved = lax.dot_general(keep[...], block[:, cut:], NT, preferred_element_type=jnp.float32)
        second_ref[:, :size] = moved.astype(jnp.bfloat16)
        return dot(left, block)

    @pl.when(k == 0)
    def _():
        row, col = iota((ranks * pitch, cut), 0), iota((ranks * pitch, cut), 1)
        pick[...] = one_hot((row % pitch < FIRST) & (col == row // pitch * FIRST + row % pitch))
        row, col = iota((ranks * pitch, roots), 0), iota((ranks * pitch, roots), 1)
        at = row % pitch - FIRST
        lay[...] = one_hot((at >= 0) & (at + core_ref[0] * half == col))
        keep[...] = one_hot(iota((aux - cut, aux - cut), 0) == iota((aux - cut, aux - cut), 1))
        sums[...] = some(CHUNK)

    @pl.when((k > 0) & (k < last))
    def _():
        sums[...] += some(CHUNK)

    @pl.when(k == last)
    def _():
        size = rows - last * CHUNK
        left_over = sums[...] + some(size)
        row, col = iota((ranks * pitch, roots), 0), iota((ranks * pitch, roots), 1)
        lay_root = one_hot(row % pitch == col)
        row, col = iota((ranks * pitch, aux), 0), iota((ranks * pitch, aux), 1)
        owner = jnp.where(col < cut, col // FIRST, (col - cut) // rest)
        mine = owner == row // pitch
        spare = CHUNK - size
        row, col = iota((aux, spare), 0), iota((aux, spare), 1)
        slot = jnp.where(row < cut, row % FIRST, FIRST + (row - cut) % rest)
        extra = jnp.zeros((ranks * pitch, spare), jnp.float32)
        for t in range(3):
            term = left_over.astype(jnp.bfloat16)
            left_over = left_over - term.astype(jnp.float32)
            spread = jnp.where(mine, dot(lay_root, term), 0.0).astype(jnp.bfloat16)
            extra = extra + dot(spread, one_hot(col == t * share + slot))
        first_ref[:, size:] = extra.astype(jnp.bfloat16)
        second_ref[:, size:] = jnp.zeros((ranks * rest, spare), jnp.bfloat16)


def pack(factors, lefts, core, dims):
    ranks, share, rows, roots = dims
    pitch = FIRST + roots // 2
    rest = share - FIRST
    steps = pl.cdiv(rows, CHUNK)
    return pl.pallas_call(
        functools.partial(pack_kernel, dims),
        grid=(steps,),
        in_specs=[
            pl.BlockSpec(memory_space=pltpu.SMEM),
            pl.BlockSpec((CHUNK, ranks * share), lambda k: (k, 0)),
            pl.BlockSpec((roots, CHUNK), lambda k: (0, k)),
        ],
        out_specs=[
            pl.BlockSpec((ranks * pitch, CHUNK), lambda k: (0, k)),
            pl.BlockSpec((ranks * rest, CHUNK), lambda k: (0, k)),
        ],
        out_shape=[
            jax.ShapeDtypeStruct((ranks * pitch, steps * CHUNK), jnp.bfloat16),
            jax.ShapeDtypeStruct((ranks * rest, steps * CHUNK), jnp.bfloat16),
        ],
        scratch_shapes=[
            pltpu.VMEM((roots, ranks * share), jnp.float32),
            pltpu.VMEM((ranks * pitch, ranks * FIRST), jnp.bfloat16),
            pltpu.VMEM((ranks * pitch, roots), jnp.bfloat16),
            pltpu.VMEM((ranks * rest, ranks * rest), jnp.bfloat16),
        ],
        compiler_params=pltpu.CompilerParams(vmem_limit_bytes=HIGH),
    )(core, factors, lefts)


def coul_kernel(dims, got_ref, send_ref, out_ref):
    ranks, share, rows, roots = dims
    pitch = FIRST + roots // 2
    rest = share - FIRST
    start = rows % LANES
    row, col = iota((roots, ranks * pitch), 0), iota((roots, ranks * pitch), 1)
    sums = dot(one_hot(col % pitch == row), got_ref[...])
    turn = LANES - share
    once = pltpu.roll(sums, turn, 1)
    sums = sums + once + pltpu.roll(once, turn, 1)
    row, col = iota((ranks * rest, roots), 0), iota((ranks * rest, roots), 1)
    laid = dot(one_hot(row % rest == col), sums.astype(jnp.bfloat16)).astype(jnp.bfloat16)
    lane = iota((ranks * rest, LANES), 1)
    out_ref[...] = jnp.where(lane < start, send_ref[...], laid)


def coul_round(got, send, dims):
    _, _, rows, _ = dims
    at = rows // LANES
    return pl.pallas_call(
        functools.partial(coul_kernel, dims),
        grid=(1,),
        in_specs=[
            pl.BlockSpec((got.shape[0], LANES), lambda k: (0, at)),
            pl.BlockSpec((send.shape[0], LANES), lambda k: (0, at)),
        ],
        out_specs=pl.BlockSpec((send.shape[0], LANES), lambda k: (0, at)),
        out_shape=jax.ShapeDtypeStruct(send.shape, send.dtype),
        input_output_aliases={1: 0},
    )(got, send)


def left_kernel(dims, got_ref, out_ref, rows):
    ranks, occ_local, vir, half = dims
    pitch = FIRST + half
    main = ranks * (occ_local - 1)
    row, col = iota((half * ranks, ranks * pitch), 0), iota((half * ranks, ranks * pitch), 1)
    turn = one_hot(col == (row % ranks) * pitch + FIRST + row // ranks)
    for i in range(occ_local):
        part = dot(turn, got_ref[:, i * vir : (i + 1) * vir]).astype(jnp.bfloat16)
        for r in range(half):
            to = r * main + i * ranks if i < occ_local - 1 else half * main + r * ranks
            rows[to : to + ranks, :] = part[r * ranks : (r + 1) * ranks]
    for at in range(0, rows.shape[0], LANES):
        out_ref[:, at : at + LANES] = rows[at : at + LANES, :].T


def left_half(got, dims):
    ranks, occ_local, vir, half = dims
    count = half * ranks * occ_local
    return pl.pallas_call(
        functools.partial(left_kernel, dims),
        in_specs=[VMEM],
        out_specs=VMEM,
        out_shape=jax.ShapeDtypeStruct((vir, count), jnp.bfloat16),
        scratch_shapes=[pltpu.VMEM((count, vir), jnp.bfloat16)],
        compiler_params=pltpu.CompilerParams(vmem_limit_bytes=24 * 1024 * 1024),
    )(got)


def to_tiles(value, out_ref):
    vir = value.shape[1]
    for t in range(out_ref.shape[0]):
        size = min(LANES, vir - t * LANES)
        out_ref[t, :, :size] = value[:, t * LANES : t * LANES + size]


def fetch_old(total_ref, old, sems):
    rows = old.shape[0]
    return pltpu.make_async_copy(total_ref.at[rows : 2 * rows, :], old, sems.at[4])


def slab_kernel(dims, final, recv_ref, mine_ref, other_ref, *refs):
    ranks, share, pitch, occ_local, vir, roots = dims
    if final:
        total_ref, give_ref, zed_ref, rows_e, left, sems, rows_z, zed, old = refs
    else:
        out_ref, left, sems, rows_z, rows_e, zed = refs
    occ = ranks * occ_local
    main = occ - ranks
    packed = main // ranks
    half = roots // 2

    @pl.when(pl.program_id(0) == 0)
    def _():
        copies = []
        for h, ref in enumerate((mine_ref, other_ref)):
            for at, size, to in (
                (0, half * main, h * half * main),
                (half * main, half * ranks, roots * main + h * half * ranks),
            ):
                copies.append(
                    pltpu.make_async_copy(
                        ref.at[:, at : at + size],
                        left.at[:, to : to + size],
                        sems.at[len(copies)],
                    )
                )
        for copy in copies:
            copy.start()
        if final:
            fetch_old(total_ref, old, sems).start()

        group = min(ranks, 256 // pitch)
        piece = group * pitch
        row, col = iota((group * share, piece), 0), iota((group * share, piece), 1)
        turn = one_hot(col == (row % group) * pitch + row // group)
        for at in range(ranks // group):
            for i in range(occ_local):
                part = recv_ref[at * piece : (at + 1) * piece, i * vir : (i + 1) * vir]
                part = dot(turn, part).astype(jnp.bfloat16)
                for s in range(share):
                    rows = part[s * group : (s + 1) * group]
                    to = s * occ + i * ranks + at * group
                    rows_z[to : to + group, :] = rows
                    if i < occ_local - 1:
                        to = s * main + i * ranks + at * group
                    else:
                        to = share * main + s * ranks + at * group
                    rows_e[to : to + group, :] = rows

        for copy in copies:
            copy.wait()
        place = iota((occ, main), 1) // ranks

        def put(r, to, value):
            if final and r < half:
                zed_ref[r * occ : (r + 1) * occ, pl.ds(to, main)] = value
            else:
                at = r - half if final else r
                zed[at * occ : (at + 1) * occ, pl.ds(to, main)] = value

        def some_vectors(k, carry):
            at = pl.multiple_of(k * packed * occ, packed * occ)
            z = dot(rows_z[pl.ds(at, packed * occ), :], left[...]).astype(jnp.bfloat16)
            for r in range(roots):
                low = roots * main + (r // packed) * main
                rest = jnp.zeros((occ, main), jnp.bfloat16)
                for s in range(packed):
                    zs = z[s * occ : (s + 1) * occ]
                    to = pl.multiple_of(k * packed * main, packed * main) + s * main
                    put(r, to, zs[:, r * main : (r + 1) * main])
                    turned = zs[:, low : low + main]
                    shift = (s - r % packed) % packed * ranks
                    if shift:
                        turned = pltpu.roll(turned, shift, 1)
                    rest = jnp.where(place == s, turned, rest)
                put(r, pl.multiple_of(share * main + k * main, main), rest)
            return carry

        lax.fori_loop(0, share // packed, some_vectors, 0)

    if final:
        part = dot(zed[...], rows_e[...])
        fetch_old(total_ref, old, sems).wait()
        to_tiles(old[:, :vir] + part, give_ref)
    else:
        step = out_ref.shape[0]
        at = pl.multiple_of(pl.program_id(0) * step, step)
        out_ref[:, :vir] = dot(zed[pl.ds(at, step), :], rows_e[...])


def slab_product(recv, mine, other, total, dims):
    ranks, share, _, occ_local, vir, roots = dims
    occ = ranks * occ_local
    width = up(vir, LANES)
    final = total is not None
    steps = 1 if final else 4
    rows = roots * occ // (2 if final else 4)
    args = [recv, mine, other] + ([total] if final else [])
    return pl.pallas_call(
        functools.partial(slab_kernel, dims, final),
        grid=(steps,),
        in_specs=[VMEM, HBM, HBM] + ([HBM] if final else []),
        out_specs=[VMEM, VMEM, VMEM] if final else pl.BlockSpec((rows, width), lambda k: (k, 0)),
        out_shape=[
            jax.ShapeDtypeStruct((width // LANES, rows, LANES), jnp.float32),
            jax.ShapeDtypeStruct((rows, share * occ), jnp.bfloat16),
            jax.ShapeDtypeStruct((share * occ, vir), jnp.bfloat16),
        ]
        if final
        else jax.ShapeDtypeStruct((roots * occ, width), jnp.float32),
        scratch_shapes=[
            pltpu.VMEM((vir, roots * occ), jnp.bfloat16),
            pltpu.SemaphoreType.DMA((5,)),
            pltpu.VMEM((share * occ, vir), jnp.bfloat16),
        ]
        + ([] if final else [pltpu.VMEM((share * occ, vir), jnp.bfloat16)])
        + [pltpu.VMEM((rows if final else roots * occ, share * occ), jnp.bfloat16)]
        + ([pltpu.VMEM((rows, width), jnp.float32)] if final else []),
        compiler_params=pltpu.CompilerParams(vmem_limit_bytes=VLIM2 if final else VLIM1),
        cost_estimate=pl.CostEstimate(
            flops=4 * share * occ * roots * occ * vir,
            transcendentals=0,
            bytes_accessed=2 * share * occ * vir + 8 * roots * occ * vir,
        ),
    )(*args)


def keep_kernel(zed_ref, rows_ref, total_ref, out_ref):
    vir = rows_ref.shape[1]
    to_tiles(total_ref[:, :vir] + dot(zed_ref[...], rows_ref[...]), out_ref)


def keep_product(zed, rows_e, total):
    rows, width = zed.shape[0], total.shape[1]
    step = rows // 2
    return pl.pallas_call(
        keep_kernel,
        grid=(2,),
        in_specs=[
            pl.BlockSpec((step, zed.shape[1]), lambda k: (k, 0)),
            VMEM,
            pl.BlockSpec((step, width), lambda k: (k, 0)),
        ],
        out_specs=pl.BlockSpec((width // LANES, step, LANES), lambda k: (0, k, 0)),
        out_shape=jax.ShapeDtypeStruct((width // LANES, rows, LANES), jnp.float32),
        compiler_params=pltpu.CompilerParams(vmem_limit_bytes=VLIM3),
        cost_estimate=pl.CostEstimate(
            flops=2 * rows * zed.shape[1] * width,
            transcendentals=0,
            bytes_accessed=8 * rows * width + 4 * rows * zed.shape[1],
        ),
    )(zed, rows_e, total)


def merge_kernel(keep_ref, other_ref, out_ref, tiles):
    ranks, occ_local, half, vir = out_ref.shape
    occ = ranks * occ_local
    for t in range(tiles.shape[0]):
        tiles[t] = keep_ref[t] + other_ref[t]
    for d in range(ranks):
        for i in range(occ_local):
            for t in range(keep_ref.shape[0]):
                at = t * LANES
                size = min(LANES, vir - at)
                rows = tiles[t, pl.ds(i * ranks + d, half, stride=occ), :]
                out_ref[d, i, :, at : at + size] = rows[:, :size].astype(jnp.bfloat16)


def merge(keep, other, shape):
    return pl.pallas_call(
        merge_kernel,
        in_specs=[VMEM, VMEM],
        out_specs=VMEM,
        out_shape=jax.ShapeDtypeStruct(shape, jnp.bfloat16),
        scratch_shapes=[pltpu.VMEM(keep.shape, jnp.float32)],
        compiler_params=pltpu.CompilerParams(vmem_limit_bytes=24 * MIB),
    )(keep, other)


def body(left_vectors, chol_factors, eps_occ, eps_vir):
    roots, occ_local, vir = left_vectors.shape
    aux_local = chol_factors.shape[2]
    ranks = lax.axis_size("pair")
    share = aux_local // ranks
    rest = share - FIRST
    rows = occ_local * vir
    half = roots // 2
    core = lax.rem(lax.axis_index("chol"), 2)
    dims = (ranks, share, rows, roots)

    lefts = jnp.pad(left_vectors.reshape(roots, rows), ((0, 0), (0, up(rows, CHUNK) - rows)))
    first_send, second_send = pack(
        chol_factors.reshape(rows, aux_local), lefts, core.reshape(1), dims
    )

    pitch = FIRST + half
    first = exchange(first_send.reshape(ranks, pitch, -1)).reshape(ranks * pitch, -1)
    second_send = coul_round(first, second_send, dims)
    second = exchange(second_send.reshape(ranks, rest, -1)).reshape(ranks * rest, -1)
    mine = left_half(first, (ranks, occ_local, vir, half))
    other = lax.ppermute(mine, "chol", CORE_SWAP)

    total = slab_product(
        first, mine, other, None, (ranks, FIRST, pitch, occ_local, vir, roots)
    )
    give, zed, rows_e = slab_product(
        second, mine, other, total, (ranks, rest, rest, occ_local, vir, roots)
    )
    got = lax.ppermute(give, "chol", CORE_SWAP)
    keep = keep_product(zed, rows_e, total)

    merged = merge(keep, got, (ranks, occ_local, half, vir))
    merged, second = lax.optimization_barrier((merged, second))
    pieces = exchange(merged)
    exch = jnp.sum(pieces.astype(jnp.float32), axis=0).transpose(1, 0, 2)

    coul_vec = second[:, rows : rows + share].reshape(ranks, roots, share).transpose(1, 0, 2)
    coul_vec = jnp.concatenate(
        [
            coul_vec[:, :, :FIRST].reshape(roots, ranks * FIRST),
            coul_vec[:, :, FIRST:].reshape(roots, ranks * rest),
        ],
        axis=1,
    )
    coulomb = jnp.einsum("iap,rp->ria", chol_factors, coul_vec, preferred_element_type=jnp.float32)
    coul_keep = lax.dynamic_slice_in_dim(coulomb, core * half, half, 0)
    coul_give = lax.dynamic_slice_in_dim(coulomb, (1 - core) * half, half, 0)
    coul_keep = coul_keep + lax.ppermute(coul_give, "chol", CORE_SWAP)

    part = 2.0 * coul_keep - exch
    part = part + lax.ppermute(part, "chol", FAR_SWAP)
    rest_part = lax.ppermute(part, "chol", CORE_SWAP)
    summed = jnp.where(
        core == 0,
        jnp.concatenate([part, rest_part], axis=0),
        jnp.concatenate([rest_part, part], axis=0),
    )
    diagonal_part = (eps_vir[None, None, :] - eps_occ[None, :, None]) * left_vectors.astype(
        jnp.float32
    )
    return diagonal_part + summed


def solution(mesh):
    placed = (P(None, "pair", None), P("pair", None, "chol"), P("pair"), P())
    return jax.shard_map(
        body, mesh=mesh, in_specs=placed, out_specs=P(None, "pair", None), check_vma=False
    )
```

```python
import functools

import jax
import jax.numpy as jnp
from jax import lax
from jax.experimental import pallas as pl
from jax.experimental.pallas import tpu as pltpu
from jax.sharding import PartitionSpec as P


CORE_SWAP = [(0, 1), (1, 0), (2, 3), (3, 2)]
FAR_SWAP = [(0, 2), (2, 0), (1, 3), (3, 1)]
LANES = 128
FIRST = 12
CHUNK = 1024
VMEM = pl.BlockSpec(memory_space=pltpu.VMEM)
ANY = pl.BlockSpec(memory_space=pl.ANY)
MIB = 1024 * 1024
HIGH = 48 * MIB
VLIM1 = 60 * MIB
VLIM2 = 44 * MIB
VLIM3 = 20 * MIB
NT = (((1,), (1,)), ((), ()))


def exchange(blocks):
    return lax.all_to_all(blocks, "pair", split_axis=0, concat_axis=0, tiled=True)


def up(value, unit):
    return pl.cdiv(value, unit) * unit


def iota(shape, axis):
    return lax.broadcasted_iota(jnp.int32, shape, axis)


def one_hot(flag):
    return jnp.where(flag, 1.0, 0.0).astype(jnp.bfloat16)


def dot(a, b):
    return jnp.dot(a, b, preferred_element_type=jnp.float32)


def pack_kernel(
    dims, core_ref, factors_ref, left_ref, first_ref, second_ref, sums, pick, lay, keep, flat
):
    ranks, share, rows, roots = dims
    half = roots // 2
    rest = share - FIRST
    pitch = FIRST + half
    cut = ranks * FIRST
    aux = ranks * share
    k = pl.program_id(0)
    last = pl.cdiv(rows, CHUNK) - 1

    def some(size):
        block = factors_ref[:size, :]
        left = flat[:, pl.ds(pl.multiple_of(k * CHUNK, CHUNK), size)]
        moved = lax.dot_general(pick[...], block[:, :cut], NT, preferred_element_type=jnp.float32)
        first_ref[:, :size] = (moved + dot(lay[...], left)).astype(jnp.bfloat16)
        moved = lax.dot_general(keep[...], block[:, cut:], NT, preferred_element_type=jnp.float32)
        second_ref[:, :size] = moved.astype(jnp.bfloat16)
        return dot(left, block)

    @pl.when(k == 0)
    def _():
        row, col = iota((ranks * pitch, cut), 0), iota((ranks * pitch, cut), 1)
        pick[...] = one_hot((row % pitch < FIRST) & (col == row // pitch * FIRST + row % pitch))
        row, col = iota((ranks * pitch, roots), 0), iota((ranks * pitch, roots), 1)
        at = row % pitch - FIRST
        lay[...] = one_hot((at >= 0) & (at + core_ref[0] * half == col))
        for i in range(left_ref.shape[0]):
            vir = left_ref.shape[2]
            flat[:, i * vir : (i + 1) * vir] = left_ref[i]
        keep[...] = one_hot(iota((aux - cut, aux - cut), 0) == iota((aux - cut, aux - cut), 1))
        sums[...] = some(CHUNK)

    @pl.when((k > 0) & (k < last))
    def _():
        sums[...] += some(CHUNK)

    @pl.when(k == last)
    def _():
        size = rows - last * CHUNK
        left_over = sums[...] + some(size)
        row, col = iota((ranks * pitch, roots), 0), iota((ranks * pitch, roots), 1)
        lay_root = one_hot(row % pitch == col)
        row, col = iota((ranks * pitch, aux), 0), iota((ranks * pitch, aux), 1)
        owner = jnp.where(col < cut, col // FIRST, (col - cut) // rest)
        mine = owner == row // pitch
        spare = CHUNK - size
        row, col = iota((aux, spare), 0), iota((aux, spare), 1)
        slot = jnp.where(row < cut, row % FIRST, FIRST + (row - cut) % rest)
        extra = jnp.zeros((ranks * pitch, spare), jnp.float32)
        for t in range(3):
            term = left_over.astype(jnp.bfloat16)
            left_over = left_over - term.astype(jnp.float32)
            spread = jnp.where(mine, dot(lay_root, term), 0.0).astype(jnp.bfloat16)
            extra = extra + dot(spread, one_hot(col == t * share + slot))
        first_ref[:, size:] = extra.astype(jnp.bfloat16)
        second_ref[:, size:] = jnp.zeros((ranks * rest, spare), jnp.bfloat16)


def pack(factors, lefts, core, dims):
    ranks, share, rows, roots = dims
    pitch = FIRST + roots // 2
    rest = share - FIRST
    steps = pl.cdiv(rows, CHUNK)
    return pl.pallas_call(
        functools.partial(pack_kernel, dims),
        grid=(steps,),
        in_specs=[
            pl.BlockSpec(memory_space=pltpu.SMEM),
            pl.BlockSpec((CHUNK, ranks * share), lambda k: (k, 0)),
            VMEM,
        ],
        out_specs=[
            pl.BlockSpec((ranks * pitch, CHUNK), lambda k: (0, k)),
            pl.BlockSpec((ranks * rest, CHUNK), lambda k: (0, k)),
        ],
        out_shape=[
            jax.ShapeDtypeStruct((ranks * pitch, steps * CHUNK), jnp.bfloat16),
            jax.ShapeDtypeStruct((ranks * rest, steps * CHUNK), jnp.bfloat16),
        ],
        scratch_shapes=[
            pltpu.VMEM((roots, ranks * share), jnp.float32),
            pltpu.VMEM((ranks * pitch, ranks * FIRST), jnp.bfloat16),
            pltpu.VMEM((ranks * pitch, roots), jnp.bfloat16),
            pltpu.VMEM((ranks * rest, ranks * rest), jnp.bfloat16),
            pltpu.VMEM((roots, steps * CHUNK), jnp.bfloat16),
        ],
        compiler_params=pltpu.CompilerParams(vmem_limit_bytes=HIGH),
    )(core, factors, lefts)


def coul_kernel(dims, got_ref, send_ref, out_ref):
    ranks, share, rows, roots = dims
    pitch = FIRST + roots // 2
    rest = share - FIRST
    start = rows % LANES
    row, col = iota((roots, ranks * pitch), 0), iota((roots, ranks * pitch), 1)
    sums = dot(one_hot(col % pitch == row), got_ref[...])
    turn = LANES - share
    once = pltpu.roll(sums, turn, 1)
    sums = sums + once + pltpu.roll(once, turn, 1)
    row, col = iota((ranks * rest, roots), 0), iota((ranks * rest, roots), 1)
    laid = dot(one_hot(row % rest == col), sums.astype(jnp.bfloat16)).astype(jnp.bfloat16)
    lane = iota((ranks * rest, LANES), 1)
    out_ref[...] = jnp.where(lane < start, send_ref[...], laid)


def coul_round(got, send, dims):
    _, _, rows, _ = dims
    at = rows // LANES
    return pl.pallas_call(
        functools.partial(coul_kernel, dims),
        grid=(1,),
        in_specs=[
            pl.BlockSpec((got.shape[0], LANES), lambda k: (0, at)),
            pl.BlockSpec((send.shape[0], LANES), lambda k: (0, at)),
        ],
        out_specs=pl.BlockSpec((send.shape[0], LANES), lambda k: (0, at)),
        out_shape=jax.ShapeDtypeStruct(send.shape, send.dtype),
        input_output_aliases={1: 0},
    )(got, send)


def left_kernel(dims, got_ref, out_ref, rows):
    ranks, occ_local, vir, half = dims
    pitch = FIRST + half
    main = ranks * (occ_local - 1)
    row, col = iota((half * ranks, ranks * pitch), 0), iota((half * ranks, ranks * pitch), 1)
    turn = one_hot(col == (row % ranks) * pitch + FIRST + row // ranks)
    for i in range(occ_local):
        part = dot(turn, got_ref[:, i * vir : (i + 1) * vir]).astype(jnp.bfloat16)
        for r in range(half):
            to = r * main + i * ranks if i < occ_local - 1 else half * main + r * ranks
            rows[to : to + ranks, :] = part[r * ranks : (r + 1) * ranks]
    for at in range(0, rows.shape[0], LANES):
        out_ref[:, at : at + LANES] = rows[at : at + LANES, :].T


def left_half(got, dims):
    ranks, occ_local, vir, half = dims
    count = half * ranks * occ_local
    return pl.pallas_call(
        functools.partial(left_kernel, dims),
        in_specs=[VMEM],
        out_specs=VMEM,
        out_shape=jax.ShapeDtypeStruct((vir, count), jnp.bfloat16),
        scratch_shapes=[pltpu.VMEM((count, vir), jnp.bfloat16)],
        compiler_params=pltpu.CompilerParams(vmem_limit_bytes=24 * 1024 * 1024),
    )(got)


def turn_rows(dims, recv_ref, rows_z, rows_e):
    ranks, share, pitch, occ_local, vir, _ = dims
    occ = ranks * occ_local
    main = occ - ranks
    group = min(ranks, 256 // pitch)
    piece = group * pitch
    row, col = iota((group * share, piece), 0), iota((group * share, piece), 1)
    turn = one_hot(col == (row % group) * pitch + row // group)
    for at in range(ranks // group):
        for i in range(occ_local):
            part = recv_ref[at * piece : (at + 1) * piece, i * vir : (i + 1) * vir]
            part = dot(turn, part).astype(jnp.bfloat16)
            for s in range(share):
                rows = part[s * group : (s + 1) * group]
                to = s * occ + i * ranks + at * group
                rows_z[to : to + group, :] = rows
                if i < occ_local - 1:
                    to = s * main + i * ranks + at * group
                else:
                    to = share * main + s * ranks + at * group
                rows_e[to : to + group, :] = rows


def fill_zed(dims, rows_z, left, zed):
    ranks, share, _, occ_local, _, roots = dims
    occ = ranks * occ_local
    main = occ - ranks
    packed = main // ranks
    place = iota((occ, main), 1) // ranks

    def some_vectors(k, carry):
        at = pl.multiple_of(k * packed * occ, packed * occ)
        z = dot(rows_z[pl.ds(at, packed * occ), :], left[...]).astype(jnp.bfloat16)
        for r in range(roots):
            low = roots * main + (r // packed) * main
            rest = jnp.zeros((occ, main), jnp.bfloat16)
            for s in range(packed):
                zs = z[s * occ : (s + 1) * occ]
                to = pl.multiple_of(k * packed * main, packed * main) + s * main
                zed[r * occ : (r + 1) * occ, pl.ds(to, main)] = zs[:, r * main : (r + 1) * main]
                turned = zs[:, low : low + main]
                shift = (s - r % packed) % packed * ranks
                if shift:
                    turned = pltpu.roll(turned, shift, 1)
                rest = jnp.where(place == s, turned, rest)
            to = pl.multiple_of(share * main + k * main, main)
            zed[r * occ : (r + 1) * occ, pl.ds(to, main)] = rest
        return carry

    lax.fori_loop(0, share // packed, some_vectors, 0)


def slab_kernel(dims, recv_ref, mine_ref, other_ref, out_ref, left, sems, rows_z, rows_e, zed):
    ranks, _, _, occ_local, vir, roots = dims
    occ = ranks * occ_local
    main = occ - ranks
    half = roots // 2

    @pl.when(pl.program_id(0) == 0)
    def _():
        copies = []
        for h, ref in enumerate((mine_ref, other_ref)):
            for at, size, to in (
                (0, half * main, h * half * main),
                (half * main, half * ranks, roots * main + h * half * ranks),
            ):
                copies.append(
                    pltpu.make_async_copy(
                        ref.at[:, at : at + size],
                        left.at[:, to : to + size],
                        sems.at[len(copies)],
                    )
                )
        for copy in copies:
            copy.start()
        turn_rows(dims, recv_ref, rows_z, rows_e)
        for copy in copies:
            copy.wait()
        fill_zed(dims, rows_z, left, zed)

    step = out_ref.shape[0]
    at = pl.multiple_of(pl.program_id(0) * step, step)
    out_ref[:, :vir] = dot(zed[pl.ds(at, step), :], rows_e[...])


def slab_product(recv, mine, other, dims):
    ranks, share, _, occ_local, vir, roots = dims
    occ = ranks * occ_local
    width = up(vir, LANES)
    steps = 4
    rows = roots * occ // steps
    return pl.pallas_call(
        functools.partial(slab_kernel, dims),
        grid=(steps,),
        in_specs=[VMEM, ANY, ANY],
        out_specs=pl.BlockSpec((rows, width), lambda k: (k, 0)),
        out_shape=jax.ShapeDtypeStruct((roots * occ, width), jnp.float32),
        scratch_shapes=[
            pltpu.VMEM((vir, roots * occ), jnp.bfloat16),
            pltpu.SemaphoreType.DMA((4,)),
            pltpu.VMEM((share * occ, vir), jnp.bfloat16),
            pltpu.VMEM((share * occ, vir), jnp.bfloat16),
            pltpu.VMEM((roots * occ, share * occ), jnp.bfloat16),
        ],
        compiler_params=pltpu.CompilerParams(vmem_limit_bytes=VLIM1),
        cost_estimate=pl.CostEstimate(
            flops=4 * share * occ * roots * occ * vir,
            transcendentals=0,
            bytes_accessed=2 * share * occ * vir + 8 * roots * occ * vir,
        ),
    )(recv, mine, other)


def half_kernel(dims, place, *refs):
    vir = dims[4]
    if place:
        recv_ref, left_ref, total_ref, out_ref, rows_z, rows_e, zed, old, sem = refs
    else:
        rows_z, rows_e, left_ref, total_ref, out_ref, zed, old, sem = refs
    rows = old.shape[0]
    fetch = pltpu.make_async_copy(total_ref.at[place * rows : (place + 1) * rows, :], old, sem)
    fetch.start()
    if place:
        turn_rows(dims, recv_ref, rows_z, rows_e)
    fill_zed(dims, rows_z, left_ref, zed)
    part = dot(zed[...], rows_e[...])
    fetch.wait()
    for t in range(out_ref.shape[0]):
        at = t * LANES
        size = min(LANES, vir - at)
        out_ref[t, :, :size] = old[:, at : at + size] + part[:, at : at + size]


def half_product(args, place, total, dims):
    ranks, share, _, occ_local, vir, roots = dims
    occ = ranks * occ_local
    rows = roots * occ
    width = up(vir, LANES)
    made = [jax.ShapeDtypeStruct((share * occ, vir), jnp.bfloat16)] * 2
    return pl.pallas_call(
        functools.partial(half_kernel, dims, place),
        in_specs=[VMEM] * len(args) + [ANY],
        out_specs=[VMEM] * (3 if place else 1),
        out_shape=[jax.ShapeDtypeStruct((width // LANES, rows, LANES), jnp.float32)]
        + (made if place else []),
        scratch_shapes=[
            pltpu.VMEM((rows, share * occ), jnp.bfloat16),
            pltpu.VMEM((rows, width), jnp.float32),
            pltpu.SemaphoreType.DMA,
        ],
        compiler_params=pltpu.CompilerParams(vmem_limit_bytes=VLIM2 if place else VLIM3),
        cost_estimate=pl.CostEstimate(
            flops=4 * share * occ * rows * vir,
            transcendentals=0,
            bytes_accessed=2 * share * occ * vir + 8 * rows * vir,
        ),
    )(*args, total)


def merge_kernel(keep_ref, other_ref, out_ref, tiles):
    ranks, occ_local, half, vir = out_ref.shape
    occ = ranks * occ_local
    for t in range(tiles.shape[0]):
        tiles[t] = keep_ref[t] + other_ref[t]
    for d in range(ranks):
        for i in range(occ_local):
            for t in range(keep_ref.shape[0]):
                at = t * LANES
                size = min(LANES, vir - at)
                rows = tiles[t, pl.ds(i * ranks + d, half, stride=occ), :]
                out_ref[d, i, :, at : at + size] = rows[:, :size].astype(jnp.bfloat16)


def merge(keep, other, shape):
    return pl.pallas_call(
        merge_kernel,
        in_specs=[VMEM, VMEM],
        out_specs=VMEM,
        out_shape=jax.ShapeDtypeStruct(shape, jnp.bfloat16),
        scratch_shapes=[pltpu.VMEM(keep.shape, jnp.float32)],
        compiler_params=pltpu.CompilerParams(vmem_limit_bytes=24 * MIB),
    )(keep, other)


def body(left_vectors, chol_factors, eps_occ, eps_vir):
    roots, occ_local, vir = left_vectors.shape
    aux_local = chol_factors.shape[2]
    ranks = lax.axis_size("pair")
    share = aux_local // ranks
    rest = share - FIRST
    rows = occ_local * vir
    half = roots // 2
    core = lax.rem(lax.axis_index("chol"), 2)
    dims = (ranks, share, rows, roots)

    first_send, second_send = pack(
        chol_factors.reshape(rows, aux_local),
        left_vectors.transpose(1, 0, 2),
        core.reshape(1),
        dims,
    )

    pitch = FIRST + half
    first = exchange(first_send.reshape(ranks, pitch, -1)).reshape(ranks * pitch, -1)
    second_send = coul_round(first, second_send, dims)
    second = exchange(second_send.reshape(ranks, rest, -1)).reshape(ranks * rest, -1)
    mine = left_half(first, (ranks, occ_local, vir, half))
    other = lax.ppermute(mine, "chol", CORE_SWAP)

    total = slab_product(first, mine, other, (ranks, FIRST, pitch, occ_local, vir, roots))
    last = (ranks, rest, rest, occ_local, vir, half)
    give, rows_z, rows_e = half_product([second, other], 1, total, last)
    got = lax.ppermute(give, "chol", CORE_SWAP)
    (keep,) = half_product([rows_z, rows_e, mine], 0, total, last)

    merged = merge(keep, got, (ranks, occ_local, half, vir))
    merged, second = lax.optimization_barrier((merged, second))
    pieces = exchange(merged)
    exch = jnp.sum(pieces.astype(jnp.float32), axis=0).transpose(1, 0, 2)

    coul_vec = second[:, rows : rows + share].reshape(ranks, roots, share).transpose(1, 0, 2)
    coul_vec = jnp.concatenate(
        [
            coul_vec[:, :, :FIRST].reshape(roots, ranks * FIRST),
            coul_vec[:, :, FIRST:].reshape(roots, ranks * rest),
        ],
        axis=1,
    )
    coulomb = jnp.einsum("iap,rp->ria", chol_factors, coul_vec, preferred_element_type=jnp.float32)
    coul_keep = lax.dynamic_slice_in_dim(coulomb, core * half, half, 0)
    coul_give = lax.dynamic_slice_in_dim(coulomb, (1 - core) * half, half, 0)
    coul_keep = coul_keep + lax.ppermute(coul_give, "chol", CORE_SWAP)

    part = 2.0 * coul_keep - exch
    part = part + lax.ppermute(part, "chol", FAR_SWAP)
    rest_part = lax.ppermute(part, "chol", CORE_SWAP)
    summed = jnp.where(
        core == 0,
        jnp.concatenate([part, rest_part], axis=0),
        jnp.concatenate([rest_part, part], axis=0),
    )
    diagonal_part = (eps_vir[None, None, :] - eps_occ[None, :, None]) * left_vectors.astype(
        jnp.float32
    )
    return diagonal_part + summed


def solution(mesh):
    placed = (P(None, "pair", None), P("pair", None, "chol"), P("pair"), P())
    return jax.shard_map(
        body, mesh=mesh, in_specs=placed, out_specs=P(None, "pair", None), check_vma=False
    )
```

```python
import functools

import jax
import jax.numpy as jnp
from jax import lax
from jax.experimental import pallas as pl
from jax.experimental.pallas import tpu as pltpu
from jax.sharding import PartitionSpec as P


CORE_SWAP = [(0, 1), (1, 0), (2, 3), (3, 2)]
FAR_SWAP = [(0, 2), (2, 0), (1, 3), (3, 1)]
LANES = 128
FIRST = 12
CHUNK = 1024
VMEM = pl.BlockSpec(memory_space=pltpu.VMEM)
ANY = pl.BlockSpec(memory_space=pl.ANY)
MIB = 1024 * 1024
HIGH = 48 * MIB
VLIM1 = 60 * MIB
VLIM2 = 44 * MIB
VLIM3 = 20 * MIB
NT = (((1,), (1,)), ((), ()))


def exchange(blocks):
    return lax.all_to_all(blocks, "pair", split_axis=0, concat_axis=0, tiled=True)


def up(value, unit):
    return pl.cdiv(value, unit) * unit


def iota(shape, axis):
    return lax.broadcasted_iota(jnp.int32, shape, axis)


def one_hot(flag):
    return jnp.where(flag, 1.0, 0.0).astype(jnp.bfloat16)


def dot(a, b):
    return jnp.dot(a, b, preferred_element_type=jnp.float32)


def pack_kernel(
    dims, core_ref, factors_ref, left_ref, first_ref, second_ref, sums, pick, flat, own
):
    ranks, share, rows, roots = dims
    half = roots // 2
    rest = share - FIRST
    pitch = FIRST + half
    cut = ranks * FIRST
    aux = ranks * share
    k = pl.program_id(0)
    last = pl.cdiv(rows, CHUNK) - 1

    def some(size):
        block = factors_ref[:size, :]
        left = flat[:, pl.ds(pl.multiple_of(k * CHUNK, CHUNK), size)]
        moved = lax.dot_general(pick[...], block[:, :cut], NT, preferred_element_type=jnp.float32)
        first_ref[:, :size] = moved.astype(jnp.bfloat16)
        mine = own[:, pl.ds(pl.multiple_of(k * CHUNK, CHUNK), size)]
        for d in range(ranks):
            first_ref[d * pitch + FIRST : (d + 1) * pitch, :size] = mine
        for at in range(0, size, LANES):
            to = min(LANES, size - at)
            second_ref[:, at : at + to] = block[at : at + to, cut:].T
        return dot(left, block)

    @pl.when(k == 0)
    def _():
        row, col = iota((ranks * pitch, cut), 0), iota((ranks * pitch, cut), 1)
        pick[...] = one_hot((row % pitch < FIRST) & (col == row // pitch * FIRST + row % pitch))
        for i in range(left_ref.shape[0]):
            vir = left_ref.shape[2]
            flat[:, i * vir : (i + 1) * vir] = left_ref[i]
        own[...] = jnp.where(core_ref[0] == 0, flat[:half, :], flat[half:, :])
        sums[...] = some(CHUNK)

    @pl.when((k > 0) & (k < last))
    def _():
        sums[...] += some(CHUNK)

    @pl.when(k == last)
    def _():
        size = rows - last * CHUNK
        left_over = sums[...] + some(size)
        row, col = iota((ranks * pitch, roots), 0), iota((ranks * pitch, roots), 1)
        lay_root = one_hot(row % pitch == col)
        row, col = iota((ranks * pitch, aux), 0), iota((ranks * pitch, aux), 1)
        owner = jnp.where(col < cut, col // FIRST, (col - cut) // rest)
        mine = owner == row // pitch
        spare = CHUNK - size
        row, col = iota((aux, spare), 0), iota((aux, spare), 1)
        slot = jnp.where(row < cut, row % FIRST, FIRST + (row - cut) % rest)
        extra = jnp.zeros((ranks * pitch, spare), jnp.float32)
        for t in range(3):
            term = left_over.astype(jnp.bfloat16)
            left_over = left_over - term.astype(jnp.float32)
            spread = jnp.where(mine, dot(lay_root, term), 0.0).astype(jnp.bfloat16)
            extra = extra + dot(spread, one_hot(col == t * share + slot))
        first_ref[:, size:] = extra.astype(jnp.bfloat16)
        second_ref[:, size:] = jnp.zeros((ranks * rest, spare), jnp.bfloat16)


def pack(factors, lefts, core, dims):
    ranks, share, rows, roots = dims
    pitch = FIRST + roots // 2
    rest = share - FIRST
    steps = pl.cdiv(rows, CHUNK)
    return pl.pallas_call(
        functools.partial(pack_kernel, dims),
        grid=(steps,),
        in_specs=[
            pl.BlockSpec(memory_space=pltpu.SMEM),
            pl.BlockSpec((CHUNK, ranks * share), lambda k: (k, 0)),
            VMEM,
        ],
        out_specs=[
            pl.BlockSpec((ranks * pitch, CHUNK), lambda k: (0, k)),
            pl.BlockSpec((ranks * rest, CHUNK), lambda k: (0, k)),
        ],
        out_shape=[
            jax.ShapeDtypeStruct((ranks * pitch, steps * CHUNK), jnp.bfloat16),
            jax.ShapeDtypeStruct((ranks * rest, steps * CHUNK), jnp.bfloat16),
        ],
        scratch_shapes=[
            pltpu.VMEM((roots, ranks * share), jnp.float32),
            pltpu.VMEM((ranks * pitch, ranks * FIRST), jnp.bfloat16),
            pltpu.VMEM((roots, steps * CHUNK), jnp.bfloat16),
            pltpu.VMEM((roots // 2, steps * CHUNK), jnp.bfloat16),
        ],
        compiler_params=pltpu.CompilerParams(vmem_limit_bytes=HIGH),
    )(core, factors, lefts)


def coul_kernel(dims, got_ref, send_ref, out_ref):
    ranks, share, rows, roots = dims
    pitch = FIRST + roots // 2
    rest = share - FIRST
    start = rows % LANES
    row, col = iota((roots, ranks * pitch), 0), iota((roots, ranks * pitch), 1)
    sums = dot(one_hot(col % pitch == row), got_ref[...])
    turn = LANES - share
    once = pltpu.roll(sums, turn, 1)
    sums = sums + once + pltpu.roll(once, turn, 1)
    row, col = iota((ranks * rest, roots), 0), iota((ranks * rest, roots), 1)
    laid = dot(one_hot(row % rest == col), sums.astype(jnp.bfloat16)).astype(jnp.bfloat16)
    lane = iota((ranks * rest, LANES), 1)
    out_ref[...] = jnp.where(lane < start, send_ref[...], laid)


def coul_round(got, send, dims):
    _, _, rows, _ = dims
    at = rows // LANES
    return pl.pallas_call(
        functools.partial(coul_kernel, dims),
        grid=(1,),
        in_specs=[
            pl.BlockSpec((got.shape[0], LANES), lambda k: (0, at)),
            pl.BlockSpec((send.shape[0], LANES), lambda k: (0, at)),
        ],
        out_specs=pl.BlockSpec((send.shape[0], LANES), lambda k: (0, at)),
        out_shape=jax.ShapeDtypeStruct(send.shape, send.dtype),
        input_output_aliases={1: 0},
    )(got, send)


def left_kernel(dims, got_ref, out_ref, rows):
    ranks, occ_local, vir, half = dims
    pitch = FIRST + half
    main = ranks * (occ_local - 1)
    row, col = iota((half * ranks, ranks * pitch), 0), iota((half * ranks, ranks * pitch), 1)
    turn = one_hot(col == (row % ranks) * pitch + FIRST + row // ranks)
    for i in range(occ_local):
        part = dot(turn, got_ref[:, i * vir : (i + 1) * vir]).astype(jnp.bfloat16)
        for r in range(half):
            to = r * main + i * ranks if i < occ_local - 1 else half * main + r * ranks
            rows[to : to + ranks, :] = part[r * ranks : (r + 1) * ranks]
    for at in range(0, rows.shape[0], LANES):
        out_ref[:, at : at + LANES] = rows[at : at + LANES, :].T


def left_half(got, dims):
    ranks, occ_local, vir, half = dims
    count = half * ranks * occ_local
    return pl.pallas_call(
        functools.partial(left_kernel, dims),
        in_specs=[VMEM],
        out_specs=VMEM,
        out_shape=jax.ShapeDtypeStruct((vir, count), jnp.bfloat16),
        scratch_shapes=[pltpu.VMEM((count, vir), jnp.bfloat16)],
        compiler_params=pltpu.CompilerParams(vmem_limit_bytes=24 * 1024 * 1024),
    )(got)


def turn_rows(dims, recv_ref, rows_z, rows_e):
    ranks, share, pitch, occ_local, vir, _ = dims
    occ = ranks * occ_local
    main = occ - ranks
    group = min(ranks, 256 // pitch)
    piece = group * pitch
    row, col = iota((group * share, piece), 0), iota((group * share, piece), 1)
    turn = one_hot(col == (row % group) * pitch + row // group)
    for at in range(ranks // group):
        for i in range(occ_local):
            part = recv_ref[at * piece : (at + 1) * piece, i * vir : (i + 1) * vir]
            part = dot(turn, part).astype(jnp.bfloat16)
            for s in range(share):
                rows = part[s * group : (s + 1) * group]
                to = s * occ + i * ranks + at * group
                rows_z[to : to + group, :] = rows
                if i < occ_local - 1:
                    to = s * main + i * ranks + at * group
                else:
                    to = share * main + s * ranks + at * group
                rows_e[to : to + group, :] = rows


def fill_zed(dims, rows_z, left, zed):
    ranks, share, _, occ_local, _, roots = dims
    occ = ranks * occ_local
    main = occ - ranks
    packed = main // ranks
    place = iota((occ, main), 1) // ranks

    def some_vectors(k, carry):
        at = pl.multiple_of(k * packed * occ, packed * occ)
        z = dot(rows_z[pl.ds(at, packed * occ), :], left[...]).astype(jnp.bfloat16)
        for r in range(roots):
            low = roots * main + (r // packed) * main
            rest = jnp.zeros((occ, main), jnp.bfloat16)
            for s in range(packed):
                zs = z[s * occ : (s + 1) * occ]
                to = pl.multiple_of(k * packed * main, packed * main) + s * main
                zed[r * occ : (r + 1) * occ, pl.ds(to, main)] = zs[:, r * main : (r + 1) * main]
                turned = zs[:, low : low + main]
                shift = (s - r % packed) % packed * ranks
                if shift:
                    turned = pltpu.roll(turned, shift, 1)
                rest = jnp.where(place == s, turned, rest)
            to = pl.multiple_of(share * main + k * main, main)
            zed[r * occ : (r + 1) * occ, pl.ds(to, main)] = rest
        return carry

    lax.fori_loop(0, share // packed, some_vectors, 0)


def slab_kernel(dims, recv_ref, mine_ref, other_ref, out_ref, left, sems, rows_z, rows_e, zed):
    ranks, _, _, occ_local, vir, roots = dims
    occ = ranks * occ_local
    main = occ - ranks
    half = roots // 2

    @pl.when(pl.program_id(0) == 0)
    def _():
        copies = []
        for h, ref in enumerate((mine_ref, other_ref)):
            for at, size, to in (
                (0, half * main, h * half * main),
                (half * main, half * ranks, roots * main + h * half * ranks),
            ):
                copies.append(
                    pltpu.make_async_copy(
                        ref.at[:, at : at + size],
                        left.at[:, to : to + size],
                        sems.at[len(copies)],
                    )
                )
        for copy in copies:
            copy.start()
        turn_rows(dims, recv_ref, rows_z, rows_e)
        for copy in copies:
            copy.wait()
        fill_zed(dims, rows_z, left, zed)

    step = out_ref.shape[0]
    at = pl.multiple_of(pl.program_id(0) * step, step)
    out_ref[:, :vir] = dot(zed[pl.ds(at, step), :], rows_e[...])


def slab_product(recv, mine, other, dims):
    ranks, share, _, occ_local, vir, roots = dims
    occ = ranks * occ_local
    width = up(vir, LANES)
    steps = 4
    rows = roots * occ // steps
    return pl.pallas_call(
        functools.partial(slab_kernel, dims),
        grid=(steps,),
        in_specs=[VMEM, ANY, ANY],
        out_specs=pl.BlockSpec((rows, width), lambda k: (k, 0)),
        out_shape=jax.ShapeDtypeStruct((roots * occ, width), jnp.float32),
        scratch_shapes=[
            pltpu.VMEM((vir, roots * occ), jnp.bfloat16),
            pltpu.SemaphoreType.DMA((4,)),
            pltpu.VMEM((share * occ, vir), jnp.bfloat16),
            pltpu.VMEM((share * occ, vir), jnp.bfloat16),
            pltpu.VMEM((roots * occ, share * occ), jnp.bfloat16),
        ],
        compiler_params=pltpu.CompilerParams(vmem_limit_bytes=VLIM1),
        cost_estimate=pl.CostEstimate(
            flops=4 * share * occ * roots * occ * vir,
            transcendentals=0,
            bytes_accessed=2 * share * occ * vir + 8 * roots * occ * vir,
        ),
    )(recv, mine, other)


def half_kernel(dims, place, *refs):
    vir = dims[4]
    if place:
        recv_ref, left_ref, total_ref, out_ref, rows_z, rows_e, zed, old, sem = refs
    else:
        rows_z, rows_e, left_ref, total_ref, out_ref, zed, old, sem = refs
    rows = old.shape[0]
    fetch = pltpu.make_async_copy(total_ref.at[place * rows : (place + 1) * rows, :], old, sem)
    fetch.start()
    if place:
        turn_rows(dims, recv_ref, rows_z, rows_e)
    fill_zed(dims, rows_z, left_ref, zed)
    part = dot(zed[...], rows_e[...])
    fetch.wait()
    for t in range(out_ref.shape[0]):
        at = t * LANES
        size = min(LANES, vir - at)
        out_ref[t, :, :size] = old[:, at : at + size] + part[:, at : at + size]


def half_product(args, place, total, dims):
    ranks, share, _, occ_local, vir, roots = dims
    occ = ranks * occ_local
    rows = roots * occ
    width = up(vir, LANES)
    made = [jax.ShapeDtypeStruct((share * occ, vir), jnp.bfloat16)] * 2
    return pl.pallas_call(
        functools.partial(half_kernel, dims, place),
        in_specs=[VMEM] * len(args) + [ANY],
        out_specs=[VMEM] * (3 if place else 1),
        out_shape=[jax.ShapeDtypeStruct((width // LANES, rows, LANES), jnp.float32)]
        + (made if place else []),
        scratch_shapes=[
            pltpu.VMEM((rows, share * occ), jnp.bfloat16),
            pltpu.VMEM((rows, width), jnp.float32),
            pltpu.SemaphoreType.DMA,
        ],
        compiler_params=pltpu.CompilerParams(vmem_limit_bytes=VLIM2 if place else VLIM3),
        cost_estimate=pl.CostEstimate(
            flops=4 * share * occ * rows * vir,
            transcendentals=0,
            bytes_accessed=2 * share * occ * vir + 8 * rows * vir,
        ),
    )(*args, total)


def merge_kernel(keep_ref, other_ref, out_ref, tiles):
    ranks, occ_local, half, vir = out_ref.shape
    occ = ranks * occ_local
    for t in range(tiles.shape[0]):
        tiles[t] = keep_ref[t] + other_ref[t]
    for d in range(ranks):
        for i in range(occ_local):
            for t in range(keep_ref.shape[0]):
                at = t * LANES
                size = min(LANES, vir - at)
                rows = tiles[t, pl.ds(i * ranks + d, half, stride=occ), :]
                out_ref[d, i, :, at : at + size] = rows[:, :size].astype(jnp.bfloat16)


def merge(keep, other, shape):
    return pl.pallas_call(
        merge_kernel,
        in_specs=[VMEM, VMEM],
        out_specs=VMEM,
        out_shape=jax.ShapeDtypeStruct(shape, jnp.bfloat16),
        scratch_shapes=[pltpu.VMEM(keep.shape, jnp.float32)],
        compiler_params=pltpu.CompilerParams(vmem_limit_bytes=24 * MIB),
    )(keep, other)


def body(left_vectors, chol_factors, eps_occ, eps_vir):
    roots, occ_local, vir = left_vectors.shape
    aux_local = chol_factors.shape[2]
    ranks = lax.axis_size("pair")
    share = aux_local // ranks
    rest = share - FIRST
    rows = occ_local * vir
    half = roots // 2
    core = lax.rem(lax.axis_index("chol"), 2)
    dims = (ranks, share, rows, roots)

    first_send, second_send = pack(
        chol_factors.reshape(rows, aux_local),
        left_vectors.transpose(1, 0, 2),
        core.reshape(1),
        dims,
    )

    pitch = FIRST + half
    first = exchange(first_send.reshape(ranks, pitch, -1)).reshape(ranks * pitch, -1)
    second_send = coul_round(first, second_send, dims)
    second = exchange(second_send.reshape(ranks, rest, -1)).reshape(ranks * rest, -1)
    mine = left_half(first, (ranks, occ_local, vir, half))
    other = lax.ppermute(mine, "chol", CORE_SWAP)

    total = slab_product(first, mine, other, (ranks, FIRST, pitch, occ_local, vir, roots))
    last = (ranks, rest, rest, occ_local, vir, half)
    give, rows_z, rows_e = half_product([second, other], 1, total, last)
    got = lax.ppermute(give, "chol", CORE_SWAP)
    (keep,) = half_product([rows_z, rows_e, mine], 0, total, last)

    merged = merge(keep, got, (ranks, occ_local, half, vir))
    merged, second = lax.optimization_barrier((merged, second))
    pieces = exchange(merged)
    exch = jnp.sum(pieces.astype(jnp.float32), axis=0).transpose(1, 0, 2)

    coul_vec = second[:, rows : rows + share].reshape(ranks, roots, share).transpose(1, 0, 2)
    coul_vec = jnp.concatenate(
        [
            coul_vec[:, :, :FIRST].reshape(roots, ranks * FIRST),
            coul_vec[:, :, FIRST:].reshape(roots, ranks * rest),
        ],
        axis=1,
    )
    coulomb = jnp.einsum("iap,rp->ria", chol_factors, coul_vec, preferred_element_type=jnp.float32)
    coul_keep = lax.dynamic_slice_in_dim(coulomb, core * half, half, 0)
    coul_give = lax.dynamic_slice_in_dim(coulomb, (1 - core) * half, half, 0)
    coul_keep = coul_keep + lax.ppermute(coul_give, "chol", CORE_SWAP)

    part = 2.0 * coul_keep - exch
    part = part + lax.ppermute(part, "chol", FAR_SWAP)
    rest_part = lax.ppermute(part, "chol", CORE_SWAP)
    summed = jnp.where(
        core == 0,
        jnp.concatenate([part, rest_part], axis=0),
        jnp.concatenate([rest_part, part], axis=0),
    )
    diagonal_part = (eps_vir[None, None, :] - eps_occ[None, :, None]) * left_vectors.astype(
        jnp.float32
    )
    return diagonal_part + summed


def solution(mesh):
    placed = (P(None, "pair", None), P("pair", None, "chol"), P("pair"), P())
    return jax.shard_map(
        body, mesh=mesh, in_specs=placed, out_specs=P(None, "pair", None), check_vma=False
    )
```
